32 devices in a mesh: tm: 4 (over z), space: 8 (over y, x, core).
Axes of the slice: x: 2, y: 2, z: 4, core: 2. Of those that a mesh axis runs over, the one named last changes fastest.
Arguments:
- right_side: float32 [64, 2048, 128], P('space', 'tm'), may hold values from -3 to 3
- blocks: float32 [64, 7, 128, 128], P('space'), may hold values from -0.1875 to 0.1875
- neighbors: int32 [64, 7], P('space'), may hold values from 0 to 63, as said below
- shift_rates: float32 [4], replicated, may hold values from 5 to 8
Outputs:
- correction: float32 [64, 2048, 128], P('space', 'tm')
The draws below stay inside these ranges and needn't reach their ends.
Inputs may be any that keep to these rules, and one draw needn't show every extreme that they name: The elements form planes of 8 consecutive elements. neighbors[e, 0] = e. With q the plane of e, column 1 names an element of plane q - 1 and column 2 one of plane q + 1, cyclically over the planes; within a plane, each of these two columns names every element of the neighbouring plane exactly once. Columns 3 to 6 name elements of plane q.
All inputs are finite; a program needn't handle non-finite values.
Results may differ from the reference program's by a relative error of at most 0.0003.
Values sent between devices are 32-bit elements; how exact they have to be, the bound alone decides.
A program may use at most 128 MiB of HBM per device.

```python
import math
import jax
import jax.numpy as jnp
from jax import lax

P_SIZE = 128
L = 2048
E_DEV = 8
SWEEPS = 4
ELEMS = 64


def permuted_row(subkey):
    return jax.random.permutation(subkey, E_DEV)


def draw_neighbors(key, part):
    plane_count = ELEMS // E_DEV
    element = jnp.arange(ELEMS, dtype=jnp.int32)
    plane_of = element // E_DEV
    subkeys = jax.random.split(jax.random.fold_in(key, 11), 2 * plane_count)
    shuffles = jax.vmap(permuted_row)(subkeys).astype(jnp.int32)
    before = shuffles[:plane_count].reshape(-1)
    after = shuffles[plane_count:].reshape(-1)
    prev_plane = (plane_of - 1) % plane_count
    next_plane = (plane_of + 1) % plane_count
    column_before = prev_plane * E_DEV + before
    column_after = next_plane * E_DEV + after
    inside = jax.random.randint(jax.random.fold_in(key, 12), (ELEMS, 4), 0, E_DEV, dtype=jnp.int32)
    inside = inside + (plane_of * E_DEV)[:, None]
    return jnp.concatenate([element[:, None], column_before[:, None], column_after[:, None], inside], 1)


def levels(rng, shape, shards, smallest, top_value):
    def one(position, parts):
        draws = jax.random.uniform(jax.random.fold_in(jax.random.fold_in(rng, 6), position), (parts,), jnp.float32, smallest / len(shards), top_value / len(shards))
        return jnp.repeat(jnp.exp(draws), shape[position] // parts).reshape((-1,) + (1,) * (len(shape) - position - 1))

    factor_of = one(*shards[0])
    for cut in shards[1:]:
        factor_of = factor_of * one(*cut)
    return factor_of


def gaussian(stream_key, shape, scale, limit, cuts=(), kind=jnp.bfloat16):
    entries = scale * jax.random.normal(stream_key, shape, jnp.float32)
    if cuts:
        entries = entries * levels(stream_key, shape, cuts, -0.22, 0.18)
    return jnp.clip(entries, -limit, limit).astype(kind)


def setup_inputs(seed: int = 0) -> dict:
    key_list = jax.random.split(jax.random.key(seed), 5)
    return {
        "right_side": gaussian(key_list[0], (ELEMS, L, P_SIZE), 0.5, 3.0, ((0, 8), (1, 4)), jnp.float32),
        "blocks": gaussian(key_list[1], (ELEMS, 7, P_SIZE, P_SIZE), (7 * P_SIZE) ** -0.5, 0.1875, ((0, 8),), jnp.float32),
        "neighbors": draw_neighbors(jax.random.fold_in(key_list[4], 71), 0),
        "shift_rates": jnp.clip(jax.random.uniform(key_list[3], (SWEEPS,), jnp.float32, 5.0, 8.0), 5.0, 8.0),
    }


WRAP_WEIGHT = 0.01
DIAG_WEIGHT = 6.0
BLOCK_WEIGHT = 3.0
STEP_SCALE = 0.1
EXACT_DOTS = lax.Precision.HIGHEST


def apply_operator(values, blocks, neighbors):
    def add_slot(slot_index, running):
        taken = jnp.take(values, neighbors[:, slot_index], axis=0)
        matrix = lax.dynamic_index_in_dim(blocks, slot_index, 1, keepdims=False)
        return running + jnp.einsum("eij,elj->eli", matrix, taken, precision=EXACT_DOTS)

    summed = lax.fori_loop(0, 7, add_slot, jnp.zeros_like(values))
    return STEP_SCALE * (DIAG_WEIGHT * values + BLOCK_WEIGHT * summed)


def reference(right_side, blocks, neighbors, shift_rates):
    moments = jnp.arange(L).astype(jnp.float32)
    growth = jnp.exp(moments * (math.log(WRAP_WEIGHT) / L))
    scaled = right_side * growth[None, :, None]
    spectrum = jnp.fft.fft(scaled, axis=1)
    spec_real = jnp.real(spectrum).astype(jnp.float32)
    spec_imag = jnp.imag(spectrum).astype(jnp.float32)
    decay_root = math.exp(math.log(WRAP_WEIGHT) / L)
    phases = moments * (2.0 * math.pi / L)
    shift_real = (1.0 - decay_root * jnp.cos(phases))[None, :, None]
    shift_imag = (decay_root * jnp.sin(phases))[None, :, None]
    iter_real = jnp.zeros_like(spec_real)
    iter_imag = jnp.zeros_like(spec_real)
    for sweep_index in range(SWEEPS):
        if sweep_index == 0:
            res_real = spec_real
            res_imag = spec_imag
        else:
            res_real = spec_real - (shift_real * iter_real - shift_imag * iter_imag) - apply_operator(iter_real, blocks, neighbors)
            res_imag = spec_imag - (shift_real * iter_imag + shift_imag * iter_real) - apply_operator(iter_imag, blocks, neighbors)
        den_real = shift_real + STEP_SCALE * shift_rates[sweep_index]
        den_imag = shift_imag
        magnitude = den_real * den_real + den_imag * den_imag
        inv_real = den_real / magnitude
        inv_imag = -den_imag / magnitude
        iter_real, iter_imag = (iter_real + inv_real * res_real - inv_imag * res_imag,
                                iter_imag + inv_real * res_imag + inv_imag * res_real)
    returned = jnp.fft.ifft(lax.complex(iter_real, iter_imag), axis=1)
    return jnp.real(returned) / growth[None, :, None]
```

```python
import functools
import math

import jax
import jax.numpy as jnp
from jax import lax
from jax.sharding import PartitionSpec as P

SWEEPS = 4
WRAP_WEIGHT = 0.01
DIAG_WEIGHT = 6.0
BLOCK_WEIGHT = 3.0
STEP_SCALE = 0.1


def cyclic_filter(value, sigma):
    plane, steps, nodes = value.shape
    devices = lax.axis_size("tm")
    me = lax.axis_index("tm")
    rate = jnp.log1p(sigma)
    ids = jnp.arange(steps, dtype=jnp.float32)
    lag = ids[:, None] - ids[None, :]
    tri = jnp.where(lag >= 0, jnp.exp(-rate * (jnp.maximum(lag, 0.0) + 1.0)), 0.0)
    local = jnp.einsum("nm,emp->enp", tri, value, precision=lax.Precision.HIGH)
    ends = lax.all_gather(local[:, -1, :], "tm")
    total = jnp.zeros_like(local[:, -1, :])
    decay = jnp.exp(-rate * steps)
    for back in range(1, devices + 1):
        source = me - back
        wrap = jnp.where(source < 0, WRAP_WEIGHT, 1.0)
        total = total + wrap * decay ** (back - 1) * ends[(source + devices) % devices]
    start = total / (1.0 - WRAP_WEIGHT * decay ** devices)
    return local + jnp.exp(-rate * (ids + 1.0))[None, :, None] * start[:, None, :]


def per_device(right_side, blocks, neighbors, shift_rates):
    plane = right_side.shape[0]
    devices = lax.axis_size("space")
    up = [(i, (i + 1) % devices) for i in range(devices)]
    down = [(j, i) for i, j in up]
    local_index = neighbors % plane
    sigma = STEP_SCALE * shift_rates
    chain = [right_side]
    for j in range(SWEEPS - 1):
        z = chain[-1]
        before = lax.ppermute(z, "space", up)
        after = lax.ppermute(z, "space", down)
        taken = [z]
        taken.append(jnp.take(before, local_index[:, 1], axis=0))
        taken.append(jnp.take(after, local_index[:, 2], axis=0))
        taken += [jnp.take(z, local_index[:, s], axis=0) for s in range(3, 7)]
        prod = jnp.einsum(
            "esij,eslj->eli", blocks, jnp.stack(taken, 1), precision=lax.Precision.HIGH
        )
        chain.append((sigma[j] - STEP_SCALE * DIAG_WEIGHT) * z - STEP_SCALE * BLOCK_WEIGHT * prod)
    out = cyclic_filter(chain[-1], sigma[SWEEPS - 1])
    for j in reversed(range(SWEEPS - 1)):
        out = cyclic_filter(chain[j] + out, sigma[j])
    return out


def solution(mesh):
    return jax.shard_map(
        per_device,
        mesh=mesh,
        in_specs=(P("space", "tm", None), P("space", None, None, None), P("space", None), P()),
        out_specs=P("space", "tm", None),
        check_vma=False,
    )
```

```python
import functools
import math

import jax
import jax.numpy as jnp
from jax import lax
from jax.experimental import pallas as pl
from jax.experimental.pallas import tpu as pltpu
from jax.sharding import PartitionSpec as P

SWEEPS = 4
SLOTS = 7
CHUNKS = 4
ROWS = 8
WRAP_WEIGHT = 0.01
DIAG_WEIGHT = 6.0
BLOCK_WEIGHT = 3.0
STEP_SCALE = 0.1
MESH = pl.DeviceIdType.MESH


def split(value):
    hi = value.astype(jnp.bfloat16)
    lo = (value - hi.astype(jnp.float32)).astype(jnp.bfloat16)
    return hi, lo


def kernel(tm_size, sp_size, x_ref, blocks_ref, local_ref, coef_ref, out_ref, *scratch):
    plane, steps, nodes = x_ref.shape
    width = steps // CHUNKS
    moves = SWEEPS - 1
    zs = [x_ref] + list(scratch[:moves])
    halos = scratch[moves : moves + 2 * moves * CHUNKS]
    weights, table, gathered, own, send_sem, recv_sem, end_send, end_recv = scratch[
        moves + 2 * moves * CHUNKS :
    ]
    tm = lax.axis_index("tm")
    sp = lax.axis_index("space")
    sides = (lax.rem(sp + 1, sp_size), lax.rem(sp + sp_size - 1, sp_size))
    peers = [lax.rem(tm + r, tm_size) for r in range(1, tm_size)]

    barrier = pltpu.get_barrier_semaphore()
    for side in sides:
        pl.semaphore_signal(barrier, inc=1, device_id={"space": side}, device_id_type=MESH)
    for peer in peers:
        pl.semaphore_signal(barrier, inc=1, device_id={"tm": peer}, device_id_type=MESH)
    pl.semaphore_wait(barrier, 2 + len(peers))

    def halo(j, c, d):
        return halos[(j * CHUNKS + c) * 2 + d]

    def transfer(j, c, d):
        return pltpu.make_async_remote_copy(
            src_ref=zs[j].at[:, pl.ds(c * width, width), :],
            dst_ref=halo(j, c, d),
            send_sem=send_sem.at[j, c, d],
            recv_sem=recv_sem.at[j, c, d],
            device_id={"space": sides[d]},
            device_id_type=MESH,
        )

    for c in range(CHUNKS):
        for d in range(2):
            transfer(0, c, d).start()

    def prepare(e, _):
        for s in range(SLOTS):
            hi, lo = split((-STEP_SCALE * BLOCK_WEIGHT) * blocks_ref[e, s].T)
            weights[e, s * nodes : (s + 1) * nodes, :nodes] = hi
            weights[e, s * nodes : (s + 1) * nodes, nodes:] = lo
        return 0

    lax.fori_loop(0, plane, prepare, 0)

    rates = [coef_ref[i] for i in range(SWEEPS)]

    def cascade(inputs, states):
        states = list(states)
        above = None
        for i in reversed(range(SWEEPS)):
            total = states[i] if inputs is None else inputs[i] + states[i]
            if above is not None:
                total = total + above
            states[i] = above = rates[i] * total
        return states

    row = lax.broadcasted_iota(jnp.int32, (ROWS, nodes), 0)
    unit = [(row == i).astype(jnp.float32) for i in range(SWEEPS)]

    def respond(g, states):
        kept = []
        for _ in range(ROWS):
            states = cascade(None, states)
            kept.append(states[0])
        flat = jnp.swapaxes(jnp.stack(kept), 0, 1)
        base = pl.multiple_of(g * ROWS, ROWS)
        for j in range(SWEEPS):
            table[j, pl.ds(base, ROWS), :] = flat[j]
        return tuple(states)

    over = lax.fori_loop(0, steps // ROWS, respond, tuple(unit))
    carry_of = [[over[i][j : j + 1, :] for j in range(SWEEPS)] for i in range(SWEEPS)]

    def advance(vectors):
        result = []
        for i in range(SWEEPS):
            total = carry_of[i][i] * vectors[i]
            for j in range(i + 1, SWEEPS):
                total = total + carry_of[i][j] * vectors[j]
            result.append(total)
        return result

    around = list(over)
    for _ in range(tm_size - 1):
        around = advance(around)

    states = tuple(jnp.zeros((ROWS, nodes), jnp.float32) for _ in range(SWEEPS))
    for j in range(moves):
        diag = coef_ref[SWEEPS + j]
        for c in range(CHUNKS):
            for d in range(2):
                transfer(j, c, d).wait_recv()
            window = pl.ds(c * width, width)

            def apply(e, _):
                here = zs[j][e, window, :]
                parts = [
                    here,
                    halo(j, c, 0)[local_ref[e, 1]],
                    halo(j, c, 1)[local_ref[e, 2]],
                ] + [zs[j][local_ref[e, s], window, :] for s in range(3, SLOTS)]
                pairs = [split(part) for part in parts]
                hi = jnp.concatenate([p[0] for p in pairs], axis=1)
                lo = jnp.concatenate([p[1] for p in pairs], axis=1)
                both = jnp.dot(hi, weights[e], preferred_element_type=jnp.float32)
                both = both + jnp.dot(lo, weights[e], preferred_element_type=jnp.float32)
                zs[j + 1][e, window, :] = diag * here + both[:, :nodes] + both[:, nodes:]
                return 0

            lax.fori_loop(0, plane, apply, 0)
            if j + 1 < moves:
                for d in range(2):
                    transfer(j + 1, c, d).start()
            else:

                def scan(g, states):
                    base = pl.multiple_of(c * width + g * ROWS, ROWS)
                    here = [jnp.swapaxes(z[:, pl.ds(base, ROWS), :], 0, 1) for z in zs]
                    kept = []
                    for t in range(ROWS):
                        states = cascade([h[t] for h in here], states)
                        kept.append(states[0])
                    out_ref[:, pl.ds(base, ROWS), :] = jnp.swapaxes(jnp.stack(kept), 0, 1)
                    return tuple(states)

                states = lax.fori_loop(0, width // ROWS, scan, states)

    for i in range(SWEEPS):
        own[i] = states[i]
    ends = [
        pltpu.make_async_remote_copy(
            src_ref=own,
            dst_ref=gathered.at[r],
            send_sem=end_send.at[r],
            recv_sem=end_recv.at[r],
            device_id={"tm": peers[r]},
            device_id_type=MESH,
        )
        for r in range(tm_size - 1)
    ]
    for copy in ends:
        copy.start()
    for copy in ends:
        copy.wait()

    def enter(back):
        entered = lax.rem(tm - back + 1 + tm_size, tm_size)
        return jnp.where(entered == 0, jnp.float32(WRAP_WEIGHT), jnp.float32(1.0))

    total = [enter(tm_size) * own[i] for i in range(SWEEPS)]
    for back in range(tm_size - 1, 0, -1):
        moved = advance(total)
        total = [enter(back) * (gathered[back - 1, i] + moved[i]) for i in range(SWEEPS)]
    start = [None] * SWEEPS
    for i in reversed(range(SWEEPS)):
        value = total[i]
        for j in range(i + 1, SWEEPS):
            value = value + WRAP_WEIGHT * around[i][j : j + 1, :] * start[j]
        start[i] = value / (1.0 - WRAP_WEIGHT * around[i][i : i + 1, :])
    for e in range(plane):
        value = out_ref[e]
        for i in range(SWEEPS):
            value = value + table[i] * start[i][e : e + 1, :]
        out_ref[e] = value

    for j in range(moves):
        for c in range(CHUNKS):
            for d in range(2):
                transfer(j, c, d).wait_send()


def solution(mesh):
    tm_size, sp_size = mesh.shape["tm"], mesh.shape["space"]

    def per_device(right_side, blocks, neighbors, shift_rates):
        plane, steps, nodes = right_side.shape
        moves = SWEEPS - 1
        sigma = STEP_SCALE * shift_rates
        coef = jnp.concatenate([1.0 / (1.0 + sigma), sigma - STEP_SCALE * DIAG_WEIGHT])
        whole = pltpu.VMEM((plane, steps, nodes), jnp.float32)
        piece = pltpu.VMEM((plane, steps // CHUNKS, nodes), jnp.float32)
        dma = pltpu.SemaphoreType.DMA
        return pl.pallas_call(
            functools.partial(kernel, tm_size, sp_size),
            out_shape=jax.ShapeDtypeStruct(right_side.shape, jnp.float32),
            in_specs=[
                pl.BlockSpec(memory_space=pltpu.VMEM),
                pl.BlockSpec(memory_space=pltpu.VMEM),
                pl.BlockSpec(memory_space=pltpu.SMEM),
                pl.BlockSpec(memory_space=pltpu.SMEM),
            ],
            out_specs=pl.BlockSpec(memory_space=pltpu.VMEM),
            scratch_shapes=[whole] * moves
            + [piece] * (2 * moves * CHUNKS)
            + [
                pltpu.VMEM((plane, SLOTS * nodes, 2 * nodes), jnp.bfloat16),
                pltpu.VMEM((SWEEPS, steps, nodes), jnp.float32),
                pltpu.VMEM((tm_size - 1, SWEEPS, plane, nodes), jnp.float32),
                pltpu.VMEM((SWEEPS, plane, nodes), jnp.float32),
                dma((moves, CHUNKS, 2)),
                dma((moves, CHUNKS, 2)),
                dma((tm_size - 1,)),
                dma((tm_size - 1,)),
            ],
            compiler_params=pltpu.CompilerParams(
                collective_id=0, has_side_effects=True, vmem_limit_bytes=56 * 2**20
            ),
        )(right_side, blocks, neighbors % plane, coef)

    return jax.shard_map(
        per_device,
        mesh=mesh,
        in_specs=(P("space", "tm", None), P("space", None, None, None), P("space", None), P()),
        out_specs=P("space", "tm", None),
        check_vma=False,
    )
```

```python
import functools
import math

import jax
import jax.numpy as jnp
from jax import lax
from jax.experimental import pallas as pl
from jax.experimental.pallas import tpu as pltpu
from jax.sharding import PartitionSpec as P

SWEEPS = 4
SLOTS = 7
PIECES = (4, 4, 4, 2, 1, 1)
CHUNKS = len(PIECES)
ROWS = 8
WRAP_WEIGHT = 0.01
DIAG_WEIGHT = 6.0
BLOCK_WEIGHT = 3.0
STEP_SCALE = 0.1
MESH = pl.DeviceIdType.MESH


def split(value):
    hi = value.astype(jnp.bfloat16)
    lo = (value - hi.astype(jnp.float32)).astype(jnp.bfloat16)
    return hi, lo


def windows(steps):
    unit = steps // sum(PIECES)
    return [(unit * sum(PIECES[:c]), unit * PIECES[c]) for c in range(CHUNKS)]


def kernel(
    tm_size, sp_size, x_ref, blocks_ref, near_ref, shift_ref,
    series_ref, table_ref, start_ref, *scratch
):
    plane, steps, nodes = x_ref.shape
    spans = windows(steps)
    moves = SWEEPS - 1
    zs = list(scratch[:SWEEPS])
    halos = scratch[SWEEPS : SWEEPS + 2 * moves * CHUNKS]
    (series, held, weights, table, gathered, own,
     send_sem, recv_sem, end_send, end_recv, load_sem, store_sem) = scratch[
        SWEEPS + 2 * moves * CHUNKS :
    ]
    tm = lax.axis_index("tm")
    sp = lax.axis_index("space")
    sides = (lax.rem(sp + 1, sp_size), lax.rem(sp + sp_size - 1, sp_size))
    peers = [lax.rem(tm + r, tm_size) for r in range(1, tm_size)]

    barrier = pltpu.get_barrier_semaphore()
    for side in sides:
        pl.semaphore_signal(barrier, inc=1, device_id={"space": side}, device_id_type=MESH)
    for peer in peers:
        pl.semaphore_signal(barrier, inc=1, device_id={"tm": peer}, device_id_type=MESH)
    load_blocks = pltpu.make_async_copy(blocks_ref, held, load_sem.at[0])
    load_x = pltpu.make_async_copy(x_ref, zs[0], load_sem.at[1])
    load_blocks.start()
    load_x.start()
    pl.semaphore_wait(barrier, 2 + len(peers))

    def near(e, s):
        return lax.rem(near_ref[e, s], plane)

    def halo(j, c, d):
        return halos[(j * CHUNKS + c) * 2 + d]

    def transfer(j, c, d):
        return pltpu.make_async_remote_copy(
            src_ref=(x_ref if j == 0 else zs[j]).at[:, pl.ds(*spans[c]), :],
            dst_ref=halo(j, c, d),
            send_sem=send_sem.at[j, c, d],
            recv_sem=recv_sem.at[j, c, d],
            device_id={"space": sides[d]},
            device_id_type=MESH,
        )

    for c in range(CHUNKS):
        for d in range(2):
            transfer(0, c, d).start()

    load_blocks.wait()

    def prepare(e, _):
        for s in range(SLOTS):
            hi, lo = split((-STEP_SCALE * BLOCK_WEIGHT) * held[e, s].T)
            weights[e, s * nodes : (s + 1) * nodes, :nodes] = hi
            weights[e, s * nodes : (s + 1) * nodes, nodes:] = lo
        return 0

    lax.fori_loop(0, plane, prepare, 0)

    sigmas = [STEP_SCALE * shift_ref[i] for i in range(SWEEPS)]
    rates = [1.0 / (1.0 + jnp.full((ROWS, nodes), sigma, jnp.float32)) for sigma in sigmas]

    def cascade(inputs, states):
        states = list(states)
        above = None
        for i in reversed(range(SWEEPS)):
            total = states[i] if inputs is None else inputs[i] + states[i]
            if above is not None:
                total = total + above
            states[i] = above = rates[i] * total
        return states

    row = lax.broadcasted_iota(jnp.int32, (ROWS, nodes), 0)
    unit = [(row == i).astype(jnp.float32) for i in range(SWEEPS)]

    def respond(g, states):
        kept = []
        for _ in range(ROWS):
            states = cascade(None, states)
            kept.append(states[0])
        flat = jnp.swapaxes(jnp.stack(kept), 0, 1)
        base = pl.multiple_of(g * ROWS, ROWS)
        for j in range(SWEEPS):
            table[j, pl.ds(base, ROWS), :] = flat[j]
        return tuple(states)

    over = lax.fori_loop(0, steps // ROWS, respond, tuple(unit))
    save_table = pltpu.make_async_copy(table, table_ref, store_sem.at[CHUNKS])
    save_table.start()
    carry_of = [[over[i][j : j + 1, :] for j in range(SWEEPS)] for i in range(SWEEPS)]

    def advance(vectors):
        result = []
        for i in range(SWEEPS):
            total = carry_of[i][i] * vectors[i]
            for j in range(i + 1, SWEEPS):
                total = total + carry_of[i][j] * vectors[j]
            result.append(total)
        return result

    around = list(over)
    for _ in range(tm_size - 1):
        around = advance(around)

    load_x.wait()
    def save(c):
        window = pl.ds(*spans[c])
        return pltpu.make_async_copy(
            series.at[:, window, :], series_ref.at[:, window, :], store_sem.at[c]
        )

    states = tuple(jnp.zeros((ROWS, nodes), jnp.float32) for _ in range(SWEEPS))
    for j in range(moves):
        diag = sigmas[j] - STEP_SCALE * DIAG_WEIGHT
        for c in range(CHUNKS):
            for d in range(2):
                transfer(j, c, d).wait_recv()
            first, width = spans[c]
            window = pl.ds(first, width)

            def apply(e, _):
                here = zs[j][e, window, :]
                parts = [
                    here,
                    halo(j, c, 0)[near(e, 1)],
                    halo(j, c, 1)[near(e, 2)],
                ] + [zs[j][near(e, s), window, :] for s in range(3, SLOTS)]
                pairs = [split(part) for part in parts]
                hi = jnp.concatenate([p[0] for p in pairs], axis=1)
                lo = jnp.concatenate([p[1] for p in pairs], axis=1)
                both = jnp.dot(hi, weights[e], preferred_element_type=jnp.float32)
                both = both + jnp.dot(lo, weights[e], preferred_element_type=jnp.float32)
                zs[j + 1][e, window, :] = diag * here + both[:, :nodes] + both[:, nodes:]
                return 0

            lax.fori_loop(0, plane, apply, 0)
            if j + 1 < moves:
                for d in range(2):
                    transfer(j + 1, c, d).start()
            else:

                def scan(g, states):
                    base = pl.multiple_of(first + g * ROWS, ROWS)
                    here = [jnp.swapaxes(z[:, pl.ds(base, ROWS), :], 0, 1) for z in zs]
                    kept = []
                    for t in range(ROWS):
                        states = cascade([h[t] for h in here], states)
                        kept.append(states[0])
                    series[:, pl.ds(base, ROWS), :] = jnp.swapaxes(jnp.stack(kept), 0, 1)
                    return tuple(states)

                states = lax.fori_loop(0, width // ROWS, scan, states)
                save(c).start()

    for i in range(SWEEPS):
        own[i] = states[i]
    ends = [
        pltpu.make_async_remote_copy(
            src_ref=own,
            dst_ref=gathered.at[r],
            send_sem=end_send.at[r],
            recv_sem=end_recv.at[r],
            device_id={"tm": peers[r]},
            device_id_type=MESH,
        )
        for r in range(tm_size - 1)
    ]
    for copy in ends:
        copy.start()
    for copy in ends:
        copy.wait()

    def enter(back):
        entered = lax.rem(tm - back + 1 + tm_size, tm_size)
        return jnp.where(entered == 0, jnp.float32(WRAP_WEIGHT), jnp.float32(1.0))

    total = [enter(tm_size) * own[i] for i in range(SWEEPS)]
    for back in range(tm_size - 1, 0, -1):
        moved = advance(total)
        total = [enter(back) * (gathered[back - 1, i] + moved[i]) for i in range(SWEEPS)]
    start = [None] * SWEEPS
    for i in reversed(range(SWEEPS)):
        value = total[i]
        for j in range(i + 1, SWEEPS):
            value = value + WRAP_WEIGHT * around[i][j : j + 1, :] * start[j]
        start[i] = value / (1.0 - WRAP_WEIGHT * around[i][i : i + 1, :])
    for e in range(plane):
        for i in range(SWEEPS):
            start_ref[e, i : i + 1, :] = start[i][e : e + 1, :]

    save_table.wait()
    for c in range(CHUNKS):
        save(c).wait()
    for j in range(moves):
        for c in range(CHUNKS):
            for d in range(2):
                transfer(j, c, d).wait_send()


def finish(series_ref, table_ref, start_ref, out_ref):
    value = series_ref[0]
    for i in range(SWEEPS):
        value = value + table_ref[i] * start_ref[0, i : i + 1, :]
    out_ref[0] = value


def solution(mesh):
    tm_size, sp_size = mesh.shape["tm"], mesh.shape["space"]

    def per_device(right_side, blocks, neighbors, shift_rates):
        plane, steps, nodes = right_side.shape
        moves = SWEEPS - 1
        f32 = jnp.float32
        whole = pltpu.VMEM((plane, steps, nodes), f32)
        pieces = [pltpu.VMEM((plane, width, nodes), f32) for _, width in windows(steps)]
        dma = pltpu.SemaphoreType.DMA
        series, table, start = pl.pallas_call(
            functools.partial(kernel, tm_size, sp_size),
            out_shape=(
                jax.ShapeDtypeStruct(right_side.shape, f32),
                jax.ShapeDtypeStruct((SWEEPS, steps, nodes), f32),
                jax.ShapeDtypeStruct((plane, SWEEPS, nodes), f32),
            ),
            in_specs=[
                pl.BlockSpec(memory_space=pl.ANY),
                pl.BlockSpec(memory_space=pl.ANY),
                pl.BlockSpec(memory_space=pltpu.SMEM),
                pl.BlockSpec(memory_space=pltpu.SMEM),
            ],
            out_specs=(
                pl.BlockSpec(memory_space=pl.ANY),
                pl.BlockSpec(memory_space=pl.ANY),
                pl.BlockSpec(memory_space=pltpu.VMEM),
            ),
            scratch_shapes=[whole] * SWEEPS
            + [piece for _ in range(moves) for piece in pieces for _ in range(2)]
            + [
                whole,
                pltpu.VMEM(blocks.shape, f32),
                pltpu.VMEM((plane, SLOTS * nodes, 2 * nodes), jnp.bfloat16),
                pltpu.VMEM((SWEEPS, steps, nodes), f32),
                pltpu.VMEM((tm_size - 1, SWEEPS, plane, nodes), f32),
                pltpu.VMEM((SWEEPS, plane, nodes), f32),
                dma((moves, CHUNKS, 2)),
                dma((moves, CHUNKS, 2)),
                dma((tm_size - 1,)),
                dma((tm_size - 1,)),
                dma((2,)),
                dma((CHUNKS + 1,)),
            ],
            compiler_params=pltpu.CompilerParams(
                collective_id=0, has_side_effects=True, vmem_limit_bytes=60 * 2**20
            ),
        )(right_side, blocks, neighbors, shift_rates)
        block = pl.BlockSpec((1, steps, nodes), lambda e: (e, 0, 0))
        return pl.pallas_call(
            finish,
            grid=(plane,),
            out_shape=jax.ShapeDtypeStruct(right_side.shape, f32),
            in_specs=[
                block,
                pl.BlockSpec((SWEEPS, steps, nodes), lambda e: (0, 0, 0)),
                pl.BlockSpec((1, SWEEPS, nodes), lambda e: (e, 0, 0)),
            ],
            out_specs=block,
        )(series, table, start)

    return jax.shard_map(
        per_device,
        mesh=mesh,
        in_specs=(P("space", "tm", None), P("space", None, None, None), P("space", None), P()),
        out_specs=P("space", "tm", None),
        check_vma=False,
    )
```

```python
import functools
import math

import jax
import jax.numpy as jnp
from jax import lax
from jax.experimental import pallas as pl
from jax.experimental.pallas import tpu as pltpu
from jax.sharding import PartitionSpec as P

SWEEPS = 4
SLOTS = 7
PIECES = (4, 4, 4, 2, 1, 1)
CHUNKS = len(PIECES)
ROWS = 8
WRAP_WEIGHT = 0.01
DIAG_WEIGHT = 6.0
BLOCK_WEIGHT = 3.0
STEP_SCALE = 0.1
MESH = pl.DeviceIdType.MESH


def split(value):
    hi = value.astype(jnp.bfloat16)
    lo = (value - hi.astype(jnp.float32)).astype(jnp.bfloat16)
    return hi, lo


def windows(steps):
    unit = steps // sum(PIECES)
    return [(unit * sum(PIECES[:c]), unit * PIECES[c]) for c in range(CHUNKS)]


def kernel(
    tm_size, sp_size, x_ref, blocks_ref, near_ref, shift_ref,
    series_ref, table_ref, start_ref, *scratch
):
    plane, steps, nodes = x_ref.shape
    spans = windows(steps)
    moves = SWEEPS - 1
    zs = list(scratch[:SWEEPS])
    halos = scratch[SWEEPS : SWEEPS + 2 * moves * CHUNKS]
    (series, held, weights, table, gathered, own,
     send_sem, recv_sem, end_send, end_recv, load_sem, store_sem) = scratch[
        SWEEPS + 2 * moves * CHUNKS :
    ]
    tm = lax.axis_index("tm")
    sp = lax.axis_index("space")
    sides = (lax.rem(sp + 1, sp_size), lax.rem(sp + sp_size - 1, sp_size))
    peers = [lax.rem(tm + r, tm_size) for r in range(1, tm_size)]

    barrier = pltpu.get_barrier_semaphore()
    for side in sides:
        pl.semaphore_signal(barrier, inc=1, device_id={"space": side}, device_id_type=MESH)
    for peer in peers:
        pl.semaphore_signal(barrier, inc=1, device_id={"tm": peer}, device_id_type=MESH)
    load_blocks = pltpu.make_async_copy(blocks_ref, held, load_sem.at[0])
    load_x = pltpu.make_async_copy(x_ref, zs[0], load_sem.at[1])
    load_blocks.start()
    load_x.start()
    pl.semaphore_wait(barrier, 2 + len(peers))

    def near(e, s):
        return lax.rem(near_ref[e, s], plane)

    def halo(j, c, d):
        return halos[(j * CHUNKS + c) * 2 + d]

    def transfer(j, c, d):
        return pltpu.make_async_remote_copy(
            src_ref=(x_ref if j == 0 else zs[j]).at[:, pl.ds(*spans[c]), :],
            dst_ref=halo(j, c, d),
            send_sem=send_sem.at[j, c, d],
            recv_sem=recv_sem.at[j, c, d],
            device_id={"space": sides[d]},
            device_id_type=MESH,
        )

    for c in range(CHUNKS):
        for d in range(2):
            transfer(0, c, d).start()

    load_blocks.wait()

    def prepare(e, _):
        for s in range(SLOTS):
            hi, lo = split((-STEP_SCALE * BLOCK_WEIGHT) * held[e, s].T)
            weights[e, s * nodes : (s + 1) * nodes, :nodes] = hi
            weights[e, s * nodes : (s + 1) * nodes, nodes:] = lo
        return 0

    lax.fori_loop(0, plane, prepare, 0)

    sigmas = [STEP_SCALE * shift_ref[i] for i in range(SWEEPS)]
    rates = [1.0 / (1.0 + jnp.full((ROWS, nodes), sigma, jnp.float32)) for sigma in sigmas]

    def cascade(inputs, states):
        states = list(states)
        above = None
        for i in reversed(range(SWEEPS)):
            total = states[i] if inputs is None else inputs[i] + states[i]
            if above is not None:
                total = total + above
            states[i] = above = rates[i] * total
        return states

    row = lax.broadcasted_iota(jnp.int32, (ROWS, nodes), 0)
    unit = [(row == i).astype(jnp.float32) for i in range(SWEEPS)]

    def respond(g, states):
        kept = []
        for _ in range(ROWS):
            states = cascade(None, states)
            kept.append(states[0])
        flat = jnp.swapaxes(jnp.stack(kept), 0, 1)
        base = pl.multiple_of(g * ROWS, ROWS)
        for j in range(SWEEPS):
            table[j, pl.ds(base, ROWS), :] = flat[j]
        return tuple(states)

    over = lax.fori_loop(0, steps // ROWS, respond, tuple(unit))
    save_table = pltpu.make_async_copy(table, table_ref, store_sem.at[CHUNKS])
    save_table.start()
    carry_of = [[over[i][j : j + 1, :] for j in range(SWEEPS)] for i in range(SWEEPS)]

    def advance(vectors):
        result = []
        for i in range(SWEEPS):
            total = carry_of[i][i] * vectors[i]
            for j in range(i + 1, SWEEPS):
                total = total + carry_of[i][j] * vectors[j]
            result.append(total)
        return result

    around = list(over)
    for _ in range(tm_size - 1):
        around = advance(around)

    load_x.wait()
    def save(c):
        window = pl.ds(*spans[c])
        return pltpu.make_async_copy(
            series.at[:, window, :], series_ref.at[:, window, :], store_sem.at[c]
        )

    states = tuple(jnp.zeros((ROWS, nodes), jnp.float32) for _ in range(SWEEPS))
    for j in range(moves):
        diag = sigmas[j] - STEP_SCALE * DIAG_WEIGHT
        for c in range(CHUNKS):
            for d in range(2):
                transfer(j, c, d).wait_recv()
            first, width = spans[c]
            window = pl.ds(first, width)

            def apply(e, _):
                here = zs[j][e, window, :]
                parts = [
                    here,
                    halo(j, c, 0)[near(e, 1)],
                    halo(j, c, 1)[near(e, 2)],
                ] + [zs[j][near(e, s), window, :] for s in range(3, SLOTS)]
                pairs = [split(part) for part in parts]
                hi = jnp.concatenate([p[0] for p in pairs], axis=1)
                lo = jnp.concatenate([p[1] for p in pairs], axis=1)
                both = jnp.dot(hi, weights[e], preferred_element_type=jnp.float32)
                both = both + jnp.dot(lo, weights[e], preferred_element_type=jnp.float32)
                zs[j + 1][e, window, :] = diag * here + both[:, :nodes] + both[:, nodes:]
                return 0

            lax.fori_loop(0, plane, apply, 0)
            if j + 1 < moves:
                for d in range(2):
                    transfer(j + 1, c, d).start()
            else:

                def scan(g, states):
                    base = pl.multiple_of(first + g * ROWS, ROWS)
                    here = [jnp.swapaxes(z[:, pl.ds(base, ROWS), :], 0, 1) for z in zs]
                    kept = []
                    for t in range(ROWS):
                        states = cascade([h[t] for h in here], states)
                        kept.append(states[0])
                    series[:, pl.ds(base, ROWS), :] = jnp.swapaxes(jnp.stack(kept), 0, 1)
                    return tuple(states)

                states = lax.fori_loop(0, width // ROWS, scan, states)
                save(c).start()

    for i in range(SWEEPS):
        own[i] = states[i]
    ends = [
        pltpu.make_async_remote_copy(
            src_ref=own,
            dst_ref=gathered.at[r],
            send_sem=end_send.at[r],
            recv_sem=end_recv.at[r],
            device_id={"tm": peers[r]},
            device_id_type=MESH,
        )
        for r in range(tm_size - 1)
    ]
    for copy in ends:
        copy.start()
    for copy in ends:
        copy.wait()

    def enter(back):
        entered = lax.rem(tm - back + 1 + tm_size, tm_size)
        return jnp.where(entered == 0, jnp.float32(WRAP_WEIGHT), jnp.float32(1.0))

    total = [enter(tm_size) * own[i] for i in range(SWEEPS)]
    for back in range(tm_size - 1, 0, -1):
        moved = advance(total)
        total = [enter(back) * (gathered[back - 1, i] + moved[i]) for i in range(SWEEPS)]
    start = [None] * SWEEPS
    for i in reversed(range(SWEEPS)):
        value = total[i]
        for j in range(i + 1, SWEEPS):
            value = value + WRAP_WEIGHT * around[i][j : j + 1, :] * start[j]
        start[i] = value / (1.0 - WRAP_WEIGHT * around[i][i : i + 1, :])
    for e in range(plane):
        for i in range(SWEEPS):
            start_ref[e, i : i + 1, :] = start[i][e : e + 1, :]

    save_table.wait()
    for c in range(CHUNKS):
        save(c).wait()
    for j in range(moves):
        for c in range(CHUNKS):
            for d in range(2):
                transfer(j, c, d).wait_send()


def finish(series_ref, table_ref, start_ref, out_ref):
    steps = series_ref.shape[1]

    def some(g, _):
        rows = pl.ds(pl.multiple_of(g * 4 * ROWS, 4 * ROWS), 4 * ROWS)
        lines = [table_ref[i, rows, :] for i in range(SWEEPS)]
        for e in range(series_ref.shape[0]):
            value = series_ref[e, rows, :]
            for i in range(SWEEPS):
                value = value + lines[i] * start_ref[e, i : i + 1, :]
            out_ref[e, rows, :] = value
        return 0

    lax.fori_loop(0, steps // (4 * ROWS), some, 0)


def solution(mesh):
    tm_size, sp_size = mesh.shape["tm"], mesh.shape["space"]

    def per_device(right_side, blocks, neighbors, shift_rates):
        plane, steps, nodes = right_side.shape
        moves = SWEEPS - 1
        f32 = jnp.float32
        whole = pltpu.VMEM((plane, steps, nodes), f32)
        pieces = [pltpu.VMEM((plane, width, nodes), f32) for _, width in windows(steps)]
        dma = pltpu.SemaphoreType.DMA
        series, table, start = pl.pallas_call(
            functools.partial(kernel, tm_size, sp_size),
            out_shape=(
                jax.ShapeDtypeStruct(right_side.shape, f32),
                jax.ShapeDtypeStruct((SWEEPS, steps, nodes), f32),
                jax.ShapeDtypeStruct((plane, SWEEPS, nodes), f32),
            ),
            in_specs=[
                pl.BlockSpec(memory_space=pl.ANY),
                pl.BlockSpec(memory_space=pl.ANY),
                pl.BlockSpec(memory_space=pltpu.SMEM),
                pl.BlockSpec(memory_space=pltpu.SMEM),
            ],
            out_specs=(
                pl.BlockSpec(memory_space=pl.ANY),
                pl.BlockSpec(memory_space=pl.ANY),
                pl.BlockSpec(memory_space=pltpu.VMEM),
            ),
            scratch_shapes=[whole] * SWEEPS
            + [piece for _ in range(moves) for piece in pieces for _ in range(2)]
            + [
                whole,
                pltpu.VMEM(blocks.shape, f32),
                pltpu.VMEM((plane, SLOTS * nodes, 2 * nodes), jnp.bfloat16),
                pltpu.VMEM((SWEEPS, steps, nodes), f32),
                pltpu.VMEM((tm_size - 1, SWEEPS, plane, nodes), f32),
                pltpu.VMEM((SWEEPS, plane, nodes), f32),
                dma((moves, CHUNKS, 2)),
                dma((moves, CHUNKS, 2)),
                dma((tm_size - 1,)),
                dma((tm_size - 1,)),
                dma((2,)),
                dma((CHUNKS + 1,)),
            ],
            compiler_params=pltpu.CompilerParams(
                collective_id=0, has_side_effects=True, vmem_limit_bytes=60 * 2**20
            ),
        )(right_side, blocks, neighbors, shift_rates)
        block = pl.BlockSpec((2, steps, nodes), lambda e: (e, 0, 0))
        return pl.pallas_call(
            finish,
            grid=(plane // 2,),
            out_shape=jax.ShapeDtypeStruct(right_side.shape, f32),
            in_specs=[
                block,
                pl.BlockSpec((SWEEPS, steps, nodes), lambda e: (0, 0, 0)),
                pl.BlockSpec((2, SWEEPS, nodes), lambda e: (e, 0, 0)),
            ],
            out_specs=block,
        )(series, table, start)

    return jax.shard_map(
        per_device,
        mesh=mesh,
        in_specs=(P("space", "tm", None), P("space", None, None, None), P("space", None), P()),
        out_specs=P("space", "tm", None),
        check_vma=False,
    )
```
